32 devices in a mesh: gx: 16 (over z, x, core), gy: 2 (over y).
Axes of the slice: x: 2, y: 2, z: 4, core: 2. Of those that a mesh axis runs over, the one named last changes fastest.
Arguments:
- queries: bfloat16 [64, 128, 1024], P('gx', 'gy'), may hold values from -42 to 42
- key_tokens: bfloat16 [64, 128, 1024], P('gx', 'gy'), may hold values from -6 to 6
- value_tokens: bfloat16 [64, 128, 1024], P('gx', 'gy'), may hold values from -6 to 6
- out_grad: bfloat16 [64, 128, 1024], P('gx', 'gy'), may hold values from -6 to 6
- conv_weight: float32 [9, 1024], replicated, may hold values from -0.9 to 0.9
- block_pairs: int32 [16, 2, 16, 2], P('gx', 'gy'), may hold values from 0 to 31, as said below
Outputs:
- layer_out: bfloat16 [64, 128, 1024], P('gx', 'gy')
- query_grad: bfloat16 [64, 128, 1024], P('gx', 'gy')
- key_grad: bfloat16 [64, 128, 1024], P('gx', 'gy')
- value_grad: bfloat16 [64, 128, 1024], P('gx', 'gy')
The draws below stay inside these ranges and needn't reach their ends.
Inputs may be any that keep to these rules, and one draw needn't show every extreme that they name: block_pairs[i, j, p] = (a local query block of tile (i, j), below 2; a key block of column j, which lies on tile (key block) // 2 along the first dimension). That tile is i + o modulo 16 with o one of 0, 1, -1, 4, 8, 12. Pairs may repeat.
All inputs are finite; a program needn't handle non-finite values.
Results may differ from the reference program's by a relative error of at most 0.009.
Values may be sent and summed in bfloat16 or wider, within the bound.
A program may use at most 128 MiB of HBM per device.

```python
import math
import jax
import jax.numpy as jnp
from jax import lax

H = 8
HD = 128
TX = 4
TY = 64
BLOCK = 128
PAIRS = 16
C = 1024
TILES_X = 16
TILES_Y = 2
STRIDE = 4
QB = 2
KBLK = 32
GRID_X = 64
GRID_Y = 128


def common_draw(base_key):
    key_query = jax.random.fold_in(base_key, 11)
    key_keys = jax.random.fold_in(base_key, 12)
    shape_all = (GRID_X, GRID_Y, H * HD)
    query_values = 2.0 * jnp.clip(jax.random.normal(key_query, shape_all, jnp.float32), -6.0, 6.0)
    key_values = jnp.clip(jax.random.normal(key_keys, shape_all, jnp.float32), -6.0, 6.0)
    return (query_values, key_values)


def draw_queries(key, part):
    return common_draw(key)[0].astype(jnp.bfloat16)


def draw_key_tokens(key, part):
    return common_draw(key)[1].astype(jnp.bfloat16)


def draw_block_pairs(key, part):
    key_count = jax.random.fold_in(key, 21)
    key_qblock = jax.random.fold_in(key, 22)
    key_pick = jax.random.fold_in(key, 23)
    key_local = jax.random.fold_in(key, 24)
    shape_pairs = (TILES_X, TILES_Y, PAIRS)
    live_count = jax.random.randint(key_count, (TILES_X, TILES_Y, 1), 2, PAIRS + 1)
    query_block = jax.random.randint(key_qblock, shape_pairs, 0, QB)
    offset_pick = jax.random.randint(key_pick, shape_pairs, 0, 6)
    local_block = jax.random.randint(key_local, shape_pairs, 0, QB)
    offset_table = jnp.array([0, 1, TILES_X - 1, STRIDE, 2 * STRIDE, 3 * STRIDE], dtype=jnp.int32)
    offset_values = offset_table[offset_pick]
    tile_ids = jnp.arange(TILES_X, dtype=jnp.int32).reshape(TILES_X, 1, 1)
    owner_tile = (tile_ids + offset_values) % TILES_X
    key_block = owner_tile * QB + local_block
    pair_index = jnp.arange(PAIRS, dtype=jnp.int32).reshape(1, 1, PAIRS)
    self_block = tile_ids * QB + query_block
    key_block = jnp.where(pair_index < live_count, key_block, self_block)
    first_query = jnp.full(shape_pairs, QB - 1, jnp.int32)
    first_key = (tile_ids + TILES_X - 1) % TILES_X * QB + QB - 1 + jnp.zeros(shape_pairs, jnp.int32)
    second_key = tile_ids * QB + jnp.zeros(shape_pairs, jnp.int32)
    query_block = jnp.where(pair_index == 0, first_query, jnp.where(pair_index == 1, 0, query_block))
    key_block = jnp.where(pair_index == 0, first_key, jnp.where(pair_index == 1, second_key, key_block))
    return jnp.stack((query_block, key_block), axis=3)


def shard_levels(rng, shape, split, smallest, high):
    factor_of = 1.0
    for axis_at, shards_of in split:
        heights = jax.random.uniform(jax.random.fold_in(jax.random.fold_in(rng, 6), axis_at), (shards_of,), jnp.float32, smallest / len(split), high / len(split))
        factor_of = factor_of * jnp.repeat(jnp.exp(heights), shape[axis_at] // shards_of).reshape((-1,) + (1,) * (len(shape) - 1 - axis_at))
    return factor_of


def bell_draw(own_key, shape, width, bound, shards=(), kind=jnp.bfloat16):
    values = jax.random.normal(own_key, shape, jnp.float32) * width
    if len(shards) > 0:
        values = shard_levels(own_key, shape, shards, -0.22, 0.18) * values
    return jnp.clip(values, min=-bound, max=bound).astype(kind)


def setup_inputs(seed: int = 0) -> dict:
    keys = jax.random.split(jax.random.key(seed), 7)
    queries = draw_queries(jax.random.fold_in(keys[6], 71), 0)
    key_tokens = draw_key_tokens(jax.random.fold_in(keys[6], 71), 0)
    value_tokens = bell_draw(keys[2], (GRID_X, GRID_Y, C), 1.0, 6.0, ((0, 16), (1, 2)))
    out_grad = bell_draw(keys[3], (GRID_X, GRID_Y, C), 1.0, 6.0, ((0, 16), (1, 2)))
    conv_weight = bell_draw(keys[4], (9, C), 0.15, 0.9, (), jnp.float32)
    block_pairs = draw_block_pairs(jax.random.fold_in(keys[6], 71), 0)
    return {"queries": queries, "key_tokens": key_tokens, "value_tokens": value_tokens, "out_grad": out_grad, "conv_weight": conv_weight, "block_pairs": block_pairs}


lowest_score = -1e+30

def stencil(padded, weights, direction, row_count, col_count):
    running_sum = jnp.zeros((row_count, col_count, padded.shape[2]), jnp.float32)
    for row_step in (-1, 0, 1):
        for col_step in (-1, 0, 1):
            row_first = 1 + direction * row_step
            col_first = 1 + direction * col_step
            window = padded[row_first:row_first + row_count, col_first:col_first + col_count]
            running_sum = running_sum + weights[3 * (row_step + 1) + col_step + 1] * window
    return running_sum

def reference(queries, key_tokens, value_tokens, out_grad, conv_weight, block_pairs):
    scale_factor = 1.0 / math.sqrt(HD)
    token_count = TX * TY
    offsets = jnp.array([0, 1, TILES_X - 1, STRIDE, 2 * STRIDE, 3 * STRIDE], dtype=jnp.int32)
    value_pad = jnp.pad(value_tokens.astype(jnp.float32), ((1, 1), (1, 1), (0, 0)))
    grad_pad = jnp.pad(out_grad.astype(jnp.float32), ((1, 1), (1, 1), (0, 0)))
    conv_value = stencil(value_pad, conv_weight, 1, GRID_X, GRID_Y)
    conv_back = stencil(grad_pad, conv_weight, -1, GRID_X, GRID_Y)

    def column(column_index):
        first_y = column_index * TY

        def column_strip(array):
            return lax.dynamic_slice_in_dim(array, first_y, TY, 1).reshape(TILES_X, token_count, H, HD)
        query_strip = column_strip(queries)
        key_strip = column_strip(key_tokens)
        value_strip = column_strip(value_tokens)
        grad_strip = column_strip(out_grad)
        pair_strip = lax.dynamic_index_in_dim(block_pairs, column_index, 1, keepdims=False)
        tile_ids = jnp.arange(TILES_X, dtype=jnp.int32)
        query_global = (tile_ids[:, None] * QB + pair_strip[:, :, 0]).reshape(-1)
        key_global = pair_strip[:, :, 1].reshape(-1)
        every_block = jnp.arange(KBLK, dtype=jnp.int32)
        query_onehot = (query_global[:, None] == every_block[None, :]).astype(jnp.float32)
        key_onehot = (key_global[:, None] == every_block[None, :]).astype(jnp.float32)
        counts = jnp.dot(query_onehot.T, key_onehot, precision=lax.Precision.HIGHEST, preferred_element_type=jnp.float32)
        block_allow = (counts > 0.5) | (every_block[:, None] == every_block[None, :])

        def tile_step(totals, tile_index):
            key_acc, value_acc = totals
            near_tiles = (tile_index + offsets) % TILES_X
            key_near = key_strip[near_tiles].reshape(6 * token_count, H, HD).astype(jnp.float32)
            value_near = value_strip[near_tiles].reshape(6 * token_count, H, HD).astype(jnp.float32)
            row_allow = lax.dynamic_slice_in_dim(block_allow, tile_index * QB, QB, 0)
            columns = (near_tiles[:, None] * QB + jnp.arange(QB, dtype=jnp.int32)[None, :]).reshape(-1)
            allowed = row_allow[:, columns]
            query_tile = lax.dynamic_index_in_dim(query_strip, tile_index, 0, keepdims=False).astype(jnp.float32)
            grad_tile = lax.dynamic_index_in_dim(grad_strip, tile_index, 0, keepdims=False).astype(jnp.float32)
            scores = jnp.einsum('qhd,khd->hqk', query_tile, key_near) * scale_factor
            shaped = (H, QB, BLOCK, 6 * QB, BLOCK)
            visible = jnp.broadcast_to(allowed[None, :, None, :, None], shaped).reshape(H, token_count, 6 * token_count)
            row_max = lax.optimization_barrier(jnp.max(jnp.where(visible, scores, lowest_score), axis=2))
            log_total = row_max + jnp.log(lax.optimization_barrier(jnp.sum(jnp.where(visible, jnp.exp(scores - row_max[:, :, None]), 0.0), axis=2)))
            probabilities = jnp.where(visible, jnp.exp(scores - log_total[:, :, None]), 0.0)
            weights = probabilities.astype(jnp.bfloat16).astype(jnp.float32)
            attended = jnp.einsum('hqk,khd->qhd', weights, value_near)
            grad_dot = jnp.einsum('qhd,qhd->hq', grad_tile, attended)
            prob_grad = jnp.einsum('qhd,khd->hqk', grad_tile, value_near)
            score_grad = (probabilities * (prob_grad - grad_dot[:, :, None]) * scale_factor).astype(jnp.bfloat16).astype(jnp.float32)
            dquery = jnp.einsum('hqk,khd->qhd', score_grad, key_near)
            key_part = jnp.einsum('hqk,qhd->khd', score_grad, query_tile).reshape(6, token_count, H, HD)
            value_part = jnp.einsum('hqk,qhd->khd', weights, grad_tile).reshape(6, token_count, H, HD)
            key_acc = key_acc.at[near_tiles].add(key_part)
            value_acc = value_acc.at[near_tiles].add(value_part)
            return ((key_acc, value_acc), (attended, dquery))
        zeros_acc = jnp.zeros((TILES_X, token_count, H, HD), jnp.float32)
        (key_acc, value_acc), (attended_all, dquery_all) = lax.scan(tile_step, (zeros_acc, zeros_acc), jnp.arange(TILES_X, dtype=jnp.int32))

        def to_grid(array):
            return array.reshape(GRID_X, TY, H * HD)
        return (to_grid(attended_all), to_grid(dquery_all), to_grid(key_acc), to_grid(value_acc))
    stacked = lax.map(column, jnp.arange(TILES_Y, dtype=jnp.int32))

    def assemble(array):
        return jnp.moveaxis(array, 0, 1).reshape(GRID_X, GRID_Y, H * HD)
    attended = assemble(stacked[0])
    dquery = assemble(stacked[1])
    dkey = assemble(stacked[2])
    dvalue = assemble(stacked[3])
    layer_out = (attended + conv_value).astype(jnp.bfloat16)
    value_grad = (dvalue + conv_back).astype(jnp.bfloat16)
    return (layer_out, dquery.astype(jnp.bfloat16), dkey.astype(jnp.bfloat16), value_grad)
```

```python
import functools
import math

import jax
import jax.numpy as jnp
from jax import lax
from jax.experimental import pallas as pl
from jax.experimental.pallas import tpu as pltpu
from jax.sharding import PartitionSpec as P

HD = 128
BLOCK = 128
NEG = -1e30
MESH = pl.DeviceIdType.MESH
SCALE = 1.0 / math.sqrt(HD)
LOG2E = math.log2(math.e)
F32 = jnp.float32
BF16 = jnp.bfloat16
ORDER = (2, 3, 1)


def kernel(
    n, m, tx, ty,
    q_ref, k_ref, v_ref, g_ref, w_ref, pairs_ref,
    o_ref, dq_ref, dk_ref, dv_ref,
    qg, gg, kk, vv, bias_own, bias_g, s_sc, o_acc, dk_acc, dv_acc,
    part_send, part_recv, res, gedge, slab, w_sc, pairs_sc,
    send_sem, recv_sem, local_sem,
):
    tokens = tx * ty
    blocks = tokens // BLOCK
    heads = q_ref.shape[2] // HD
    hp = heads // 4
    quarter = n // 4
    own = lax.axis_index("gx")
    col = lax.axis_index("gy")
    slot = own // quarter
    rank = lax.rem(own, quarter)
    outputs = (o_ref, dq_ref, dk_ref, dv_ref)

    def far(d):
        return {"gx": lax.rem(own + d * quarter, n)}

    next_group = {"gx": slot * quarter + lax.rem(rank + 1, quarter)}
    prev_group = {"gx": slot * quarter + lax.rem(rank + quarter - 1, quarter)}
    groups = (next_group, prev_group)
    next_col = {"gy": lax.rem(col + 1, m)}
    prev_col = {"gy": lax.rem(col + m - 1, m)}
    cols_of = (next_col, prev_col)

    barrier = pltpu.get_barrier_semaphore()
    partners = [far(1), far(2), far(3), next_group, prev_group, next_col, prev_col]
    for partner in partners:
        pl.semaphore_signal(barrier, inc=1, device_id=partner, device_id_type=MESH)

    count = [0]
    sent = []
    local_count = [0]

    def reserve(k):
        at = count[0]
        count[0] += k
        return at

    def remote(src, dst, device, at):
        return pltpu.make_async_remote_copy(
            src_ref=src, dst_ref=dst, send_sem=send_sem.at[at], recv_sem=recv_sem.at[at],
            device_id=device, device_id_type=MESH,
        )

    def send(src, dst, device):
        copy = remote(src, dst, device, reserve(1))
        copy.start()
        sent.append(copy)
        return copy

    def local(src, dst):
        copy = pltpu.make_async_copy(src, dst, local_sem.at[local_count[0]])
        local_count[0] += 1
        copy.start()
        return copy

    def head_cols(head):
        return pl.ds(pl.multiple_of(head * HD, HD), HD)

    pairs_copy = local(pairs_ref, pairs_sc)
    w_copy = local(w_ref, w_sc)
    K, V, G, Q = 0, 1, 2, 3
    arrays = ((k_ref, lambda h, s: kk.at[h, 0, s]), (v_ref, lambda h, s: vv.at[h, 0, s]),
              (g_ref, lambda h, s: gg.at[h, s]), (q_ref, lambda h, s: qg.at[h, s]))
    mine = {}
    for h in range(hp):
        for a, (ref, place) in enumerate(arrays):
            mine[h, a] = local(ref.at[:, :, head_cols(slot * hp + h)], place(h, slot))

    pl.semaphore_wait(barrier, len(partners))

    incoming = {}
    in_base = {}
    for h in range(hp):
        for a, (ref, place) in enumerate(arrays):
            in_base[h, a] = count[0]
            for d in ORDER:
                target = lax.rem(slot + d, 4)
                incoming[h, a, d] = send(ref.at[:, :, head_cols(target * hp + h)], place(h, slot), far(d))

    forwards = {}
    fwd_base = {}
    bufs = (kk, vv)
    for h in range(hp):
        for a, (ref, _) in enumerate(arrays[:2]):
            for nb in (1, 2):
                forwards[h, a, 0, nb] = send(
                    ref.at[:, :, head_cols(slot * hp + h)], bufs[a].at[h, nb, slot], groups[2 - nb])
            fwd_base[h, a] = reserve(6)

    def order_at(t):
        return lax.rem(t + 1, 3) + 1

    def forward(h, a, t):
        s = lax.rem(slot + 4 - order_at(t), 4)
        remote(bufs[a].at[h, 0, s], bufs[a].at[h, 0, s], far(1), in_base[h, a] + t).wait_recv()
        for nb in (1, 2):
            remote(bufs[a].at[h, 0, s], bufs[a].at[h, nb, s], groups[2 - nb], fwd_base[h, a] + t * 2 + nb - 1).start()

    def forwards_done(h, a, recv):
        for nb in (1, 2):
            if recv:
                forwards[h, a, 0, nb].wait_recv()
            for t in range(3):
                copy = remote(bufs[a].at[h, 0, 0], bufs[a].at[h, nb, 0], groups[2 - nb], fwd_base[h, a] + t * 2 + nb - 1)
                if recv:
                    copy.wait_recv()
                else:
                    copy.wait_send()

    pairs_copy.wait()
    query_of = pairs_sc[0:1, :]
    key_of = pairs_sc[1:2, :]
    tiles = [rank + quarter * s for s in range(4)] + [lax.rem(own + 1, n), lax.rem(own + n - 1, n)]
    bias_own[...] = jnp.full(bias_own.shape, NEG, F32)
    for j, tile in enumerate(tiles):
        for c in range(blocks):
            key_id = tile * blocks + c
            for b in range(blocks):
                hit = jnp.where((query_of == b) & (key_of == key_id), 1.0, 0.0)
                hit = jnp.max(hit, axis=1, keepdims=True)
                hit = jnp.maximum(hit, (own * blocks + b == key_id).astype(F32))
                value = jnp.where(hit > 0.5, 0.0, NEG)
                at = j * tokens + c * BLOCK
                bias_own[b:b + 1, at:at + BLOCK] = jnp.broadcast_to(value, (1, BLOCK))
    bias_copies = [send(bias_own, bias_g.at[slot], far(d)) for d in ORDER]
    bias_mine = local(bias_own, bias_g.at[slot])
    w_copy.wait()

    ahead = (rank == quarter - 1).astype(jnp.int32)
    behind = 3 * (rank == 0).astype(jnp.int32)
    halo = {0: {}, 1: {}}
    edges = {}

    def halo_main(a, h):
        buf = vv.at[h, 0] if a == 0 else gg.at[h]
        halo[a][h] = [
            send(buf.at[:, :, pl.ds(first, 16)], slab.at[a, h, side, :, pl.ds(1, tx)], cols_of[side])
            for side, first in ((0, ty - 16), (1, 0))
        ]

    def halo_edges(a, h):
        for e, x in ((1, tx + 1), (2, 0)):
            if a == 0:
                row = vv.at[h, e, :, 0 if e == 1 else tx - 1]
            else:
                row = gedge.at[h, e - 1]
            for side, first in ((0, ty - 16), (1, 0)):
                halo[a][h].append(send(row.at[:, pl.ds(first, 16)], slab.at[a, h, side, :, x], cols_of[side]))

    def arrive_v(h):
        mine[h, V].wait()
        halo_main(0, h)

    def arrive_g(h):
        for d in ORDER:
            incoming[h, G, d].wait_recv()
        mine[h, G].wait()
        edges[h] = [send(gg.at[h, :, tx - 1], gedge.at[h, 1], next_group),
                    send(gg.at[h, :, 0], gedge.at[h, 0], prev_group)]
        halo_main(1, h)

    def arrive_rest(h):
        forwards_done(h, V, True)
        halo_edges(0, h)
        for d in ORDER:
            incoming[h, Q, d].wait_recv()
        for copy in edges[h]:
            copy.wait_recv()
        halo_edges(1, h)
        forwards_done(h, K, True)
        mine[h, K].wait()
        mine[h, Q].wait()

    has_left = (col > 0).astype(F32)
    has_right = (col < m - 1).astype(F32)

    def conv_tile(a, h, i):
        tile = i * quarter + rank
        has_up = (tile > 0).astype(F32)
        has_down = (tile < n - 1).astype(F32)
        above = lax.rem(i + behind, 4)
        below = lax.rem(i + ahead, 4)
        cols = head_cols(slot * hp + h)
        row_id = lax.broadcasted_iota(jnp.int32, (ty, HD), 0)
        sums = [None] * tx
        for x in range(tx + 2):
            if x == 0:
                row = (vv[h, 2, above, tx - 1] if a == 0 else gedge[h, 1, above]).astype(F32) * has_up
                at = above
            elif x == tx + 1:
                row = (vv[h, 1, below, 0] if a == 0 else gedge[h, 0, below]).astype(F32) * has_down
                at = below
            else:
                row = (vv[h, 0, i, x - 1] if a == 0 else gg[h, i, x - 1]).astype(F32)
                at = i
            left = slab[a, h, 0, at, x].astype(F32)[15:16] * has_left
            right = slab[a, h, 1, at, x].astype(F32)[0:1] * has_right
            if x == 0:
                left, right = left * has_up, right * has_up
            if x == tx + 1:
                left, right = left * has_down, right * has_down
            shifted = (
                jnp.where(row_id == 0, left, pltpu.roll(row, 1, 0)),
                row,
                jnp.where(row_id == ty - 1, right, pltpu.roll(row, ty - 1, 0)),
            )
            for step in (-1, 0, 1):
                target = x - 1 - step
                if 0 <= target < tx:
                    for b in range(3):
                        tap = 3 * (step + 1) + b
                        tap = tap if a == 0 else 8 - tap
                        term = w_sc[pl.ds(tap, 1), cols] * shifted[b]
                        sums[target] = term if sums[target] is None else sums[target] + term
        return jnp.concatenate(sums, axis=0)

    nt = (((1,), (1,)), ((), ()))
    nn = (((1,), (0,)), ((), ()))
    tn = (((0,), (0,)), ((), ()))

    def dot(x, y, dims):
        return lax.dot_general(x, y, dims, preferred_element_type=F32)

    def flat(x):
        return x.reshape(tokens, HD)

    back_base = {}

    def give_back(a, h, t, i):
        cols = head_cols(slot * hp + h)

        @pl.when(t < 3)
        def _():
            remote(res.at[a, h, i], outputs[a].at[:, :, cols], {"gx": i * quarter + rank}, back_base[a, h] + t).start()

    def keep(a, h):
        return local(res.at[a, h, slot], outputs[a].at[:, :, head_cols(slot * hp + h)])

    part_base = {}

    def attend(h):
        back_base[1, h] = reserve(3)
        part_base[h] = reserve(16)
        dk_acc[...] = jnp.zeros(dk_acc.shape, F32)
        dv_acc[...] = jnp.zeros(dv_acc.shape, F32)

        @pl.loop(0, 4)
        def _(t):
            i = lax.rem(slot + lax.rem(t + 1, 3) + 1, 4)
            i = lax.select(t == 3, slot, i)
            q = flat(qg[h, i])
            g = flat(gg[h, i])
            keys = [(0, 0), (0, 1), (0, 2), (0, 3), (1, lax.rem(i + ahead, 4)), (2, lax.rem(i + behind, 4))]
            top = None
            for j, (nb, s) in enumerate(keys):
                js = pl.ds(j * tokens, tokens)
                score = dot(q, flat(kk[h, nb, s]), nt)
                bias = bias_g[i, :, js]
                parts = [score[b * BLOCK:(b + 1) * BLOCK] + bias[b:b + 1] for b in range(blocks)]
                score = jnp.concatenate(parts, axis=0)
                s_sc[:, js] = score
                peak = jnp.max(score, axis=1, keepdims=True)
                top = peak if top is None else jnp.maximum(top, peak)
            total = jnp.zeros((tokens, 1), F32)
            out = jnp.zeros((tokens, HD), F32)
            for j, (nb, s) in enumerate(keys):
                js = pl.ds(j * tokens, tokens)
                prob = jnp.exp2((s_sc[:, js] - top) * (SCALE * LOG2E))
                s_sc[:, js] = prob
                total = total + jnp.sum(prob, axis=1, keepdims=True)
                out = out + dot(prob.astype(BF16), flat(vv[h, nb, s]), nn)
            inv = 1.0 / total
            out = out * inv
            o_acc[i] = out
            grad_dot = jnp.sum(g.astype(F32) * out, axis=1, keepdims=True)
            dq = jnp.zeros((tokens, HD), F32)
            for j, (nb, s) in enumerate(keys):
                js = pl.ds(j * tokens, tokens)
                prob_grad = dot(g, flat(vv[h, nb, s]), nt)
                prob = s_sc[:, js] * inv
                score_grad = (prob * (prob_grad - grad_dot)).astype(BF16)
                dq = dq + dot(score_grad, flat(kk[h, nb, s]), nn)
                dk = dot(score_grad, q, tn)
                dv = dot(prob.astype(BF16), g, tn)
                if nb == 0:
                    dk_acc[s] += dk
                    dv_acc[s] += dv
                else:
                    for a, value in enumerate((dk, dv)):
                        part_send[a, h, nb - 1, s] = value.astype(BF16).reshape(tx, ty, HD)
                        remote(part_send.at[a, h, nb - 1, s], part_recv.at[a, h, nb - 1, s], groups[nb - 1],
                               part_base[h] + t * 4 + a * 2 + nb - 1).start()
            res[1, h, i] = (dq * SCALE).astype(BF16).reshape(tx, ty, HD)
            give_back(1, h, t, i)
            if h + 1 < hp:

                @pl.when(t < 3)
                def _():
                    forward(h + 1, K, t)
                    forward(h + 1, V, t)

        kept.append(keep(1, h))

    def tile_at(t):
        return lax.select(t == 3, slot, lax.rem(slot + lax.rem(t + 1, 3) + 1, 4))

    def finish_out(h):
        for copy in halo[0][h]:
            copy.wait_recv()
        back_base[0, h] = reserve(3)

        @pl.loop(0, 4)
        def _(t):
            i = tile_at(t)
            res[0, h, i] = (o_acc[i] + conv_tile(0, h, i)).astype(BF16).reshape(tx, ty, HD)
            give_back(0, h, t, i)

        kept.append(keep(0, h))

    def part_copy(h, t, a, nb):
        return remote(part_send.at[a, h, nb, 0], part_recv.at[a, h, nb, 0], groups[nb], part_base[h] + t * 4 + a * 2 + nb)

    def finish_grads(h):
        for t in range(4):
            for a in range(2):
                for nb in range(2):
                    part_copy(h, t, a, nb).wait_recv()
        for copy in halo[1][h]:
            copy.wait_recv()
        back_base[2, h] = reserve(3)
        back_base[3, h] = reserve(3)

        @pl.loop(0, 4)
        def _(t):
            s = tile_at(t)
            for a, acc in enumerate((dk_acc, dv_acc)):
                value = acc[s] + flat(part_recv[a, h, 0, s]).astype(F32) + flat(part_recv[a, h, 1, s]).astype(F32)
                value = value * SCALE if a == 0 else value + conv_tile(1, h, s)
                res[2 + a, h, s] = value.astype(BF16).reshape(tx, ty, HD)
                give_back(2 + a, h, t, s)

        kept.append(keep(2, h))
        kept.append(keep(3, h))

    kept = []
    for t in range(3):
        forward(0, K, t)
    for t in range(3):
        forward(0, V, t)
    for h in range(hp):
        arrive_v(h)
        arrive_g(h)
        arrive_rest(h)
        if h == 0:
            bias_mine.wait()
            for copy in bias_copies:
                copy.wait_recv()
        attend(h)
        finish_out(h)
        finish_grads(h)

    for copy in kept:
        copy.wait()
    for a in range(4):
        for h in range(hp):
            for t in range(3):
                copy = remote(res.at[a, h, 0], outputs[a].at[:, :, head_cols(slot * hp + h)], far(1), back_base[a, h] + t)
                copy.wait_recv()
                copy.wait_send()
    for h in range(hp):
        for a in range(2):
            forwards_done(h, a, False)
            for t in range(4):
                for nb in range(2):
                    part_copy(h, t, a, nb).wait_send()
    for copy in sent:
        copy.wait_send()


def hand_over(*refs):
    count = (len(refs) - 2) // 2
    sources, targets = refs[:count], refs[count:2 * count]
    stage, sems = refs[2 * count:]
    first = [pltpu.make_async_copy(sources[a], stage.at[a], sems.at[0, a]) for a in range(count)]
    second = [pltpu.make_async_copy(stage.at[a], targets[a], sems.at[1, a]) for a in range(count)]
    for copy in first:
        copy.start()
    for a in range(count):
        first[a].wait()
        second[a].start()
    for copy in second:
        copy.wait()


def per_device(n, m, queries, key_tokens, value_tokens, out_grad, conv_weight, block_pairs):
    tx, ty, width = queries.shape
    heads = width // HD
    hp = heads // 4
    tokens = tx * ty
    pairs = block_pairs.shape[2]
    vmem = pl.BlockSpec(memory_space=pltpu.VMEM)
    anywhere = pl.BlockSpec(memory_space=pl.ANY)
    shape = jax.ShapeDtypeStruct(queries.shape, BF16)
    outs = pl.pallas_call(
        functools.partial(kernel, n, m, tx, ty),
        out_shape=(shape,) * 4,
        in_specs=[anywhere] * 6,
        out_specs=(anywhere,) * 4,
        scratch_shapes=[
            pltpu.VMEM((hp, 4, tx, ty, HD), BF16),
            pltpu.VMEM((hp, 4, tx, ty, HD), BF16),
            pltpu.VMEM((hp, 3, 4, tx, ty, HD), BF16),
            pltpu.VMEM((hp, 3, 4, tx, ty, HD), BF16),
            pltpu.VMEM((8, 6 * tokens), F32),
            pltpu.VMEM((4, 8, 6 * tokens), F32),
            pltpu.VMEM((tokens, 6 * tokens), F32),
            pltpu.VMEM((4, tokens, HD), F32),
            pltpu.VMEM((4, tokens, HD), F32),
            pltpu.VMEM((4, tokens, HD), F32),
            pltpu.VMEM((2, hp, 2, 4, tx, ty, HD), BF16),
            pltpu.VMEM((2, hp, 2, 4, tx, ty, HD), BF16),
            pltpu.VMEM((4, hp, 4, tx, ty, HD), BF16),
            pltpu.VMEM((hp, 2, 4, ty, HD), BF16),
            pltpu.VMEM((2, hp, 2, 4, tx + 2, 16, HD), BF16),
            pltpu.VMEM((9, width), F32),
            pltpu.VMEM((2, pairs), jnp.int32),
            pltpu.SemaphoreType.DMA((160,)),
            pltpu.SemaphoreType.DMA((160,)),
            pltpu.SemaphoreType.DMA((8 * hp + 3,)),
        ],
        compiler_params=pltpu.CompilerParams(
            collective_id=0, has_side_effects=True, vmem_limit_bytes=60 * 1024 * 1024
        ),
    )(queries, key_tokens, value_tokens, out_grad, conv_weight, block_pairs[0, 0].T)
    return pl.pallas_call(
        hand_over,
        out_shape=(shape,) * 4,
        in_specs=[anywhere] * 4,
        out_specs=(anywhere,) * 4,
        scratch_shapes=[pltpu.VMEM((4, tx, ty, width), BF16), pltpu.SemaphoreType.DMA((2, 4))],
    )(*outs)


def solution(mesh):
    grid = P("gx", "gy", None)
    return jax.shard_map(
        functools.partial(per_device, mesh.shape["gx"], mesh.shape["gy"]),
        mesh=mesh,
        in_specs=(grid, grid, grid, grid, P(), P("gx", "gy", None, None)),
        out_specs=(grid, grid, grid, grid),
        check_vma=False,
    )
```

```python
import functools
import math

import jax
import jax.numpy as jnp
from jax import lax
from jax.experimental import pallas as pl
from jax.experimental.pallas import tpu as pltpu
from jax.sharding import PartitionSpec as P

HD = 128
BLOCK = 128
NEG = -1e30
MESH = pl.DeviceIdType.MESH
SCALE = 1.0 / math.sqrt(HD)
LOG2E = math.log2(math.e)
F32 = jnp.float32
BF16 = jnp.bfloat16
ORDER = (2, 3, 1)


def kernel(
    n, m, tx, ty,
    q_ref, k_ref, v_ref, g_ref, w_ref, pairs_ref,
    o_ref, dq_ref, dk_ref, dv_ref,
    qg, gg, kk, vv, bias_g, s_sc, o_acc, dk_acc, dv_acc,
    part_send, part_recv, res, gedge, slab, w_sc, pairs_sc,
    send_sem, recv_sem, local_sem,
):
    tokens = tx * ty
    blocks = tokens // BLOCK
    heads = q_ref.shape[2] // HD
    hp = heads // 4
    quarter = n // 4
    own = lax.axis_index("gx")
    col = lax.axis_index("gy")
    slot = own // quarter
    rank = lax.rem(own, quarter)
    outputs = (o_ref, dq_ref, dk_ref, dv_ref)

    def far(d):
        return {"gx": lax.rem(own + d * quarter, n)}

    next_group = {"gx": slot * quarter + lax.rem(rank + 1, quarter)}
    prev_group = {"gx": slot * quarter + lax.rem(rank + quarter - 1, quarter)}
    groups = (next_group, prev_group)
    next_col = {"gy": lax.rem(col + 1, m)}
    prev_col = {"gy": lax.rem(col + m - 1, m)}
    cols_of = (next_col, prev_col)

    barrier = pltpu.get_barrier_semaphore()
    partners = [far(1), far(2), far(3), next_group, prev_group, next_col, prev_col]
    for partner in partners:
        pl.semaphore_signal(barrier, inc=1, device_id=partner, device_id_type=MESH)

    count = [0]
    sent = []
    local_count = [0]

    def reserve(k):
        at = count[0]
        count[0] += k
        return at

    def remote(src, dst, device, at):
        return pltpu.make_async_remote_copy(
            src_ref=src, dst_ref=dst, send_sem=send_sem.at[at], recv_sem=recv_sem.at[at],
            device_id=device, device_id_type=MESH,
        )

    def send(src, dst, device):
        copy = remote(src, dst, device, reserve(1))
        copy.start()
        sent.append(copy)
        return copy

    def local(src, dst):
        copy = pltpu.make_async_copy(src, dst, local_sem.at[local_count[0]])
        local_count[0] += 1
        copy.start()
        return copy

    def head_cols(head):
        return pl.ds(pl.multiple_of(head * HD, HD), HD)

    pairs_copy = local(pairs_ref, pairs_sc.at[slot])
    w_copy = local(w_ref, w_sc)
    K, V, G, Q = 0, 1, 2, 3
    arrays = ((k_ref, lambda h, s: kk.at[h, 0, s]), (v_ref, lambda h, s: vv.at[h, 0, s]),
              (g_ref, lambda h, s: gg.at[h, s]), (q_ref, lambda h, s: qg.at[h, s]))
    mine = {}
    for h in range(hp):
        for a, (ref, place) in enumerate(arrays):
            mine[h, a] = local(ref.at[:, :, head_cols(slot * hp + h)], place(h, slot))

    pl.semaphore_wait(barrier, len(partners))

    pairs_copies = [send(pairs_ref, pairs_sc.at[slot], far(d)) for d in ORDER]
    incoming = {}
    in_base = {}
    for h in range(hp):
        for a, (ref, place) in enumerate(arrays):
            in_base[h, a] = count[0]
            for d in ORDER:
                target = lax.rem(slot + d, 4)
                incoming[h, a, d] = send(ref.at[:, :, head_cols(target * hp + h)], place(h, slot), far(d))

    forwards = {}
    fwd_base = {}
    bufs = (kk, vv)
    for h in range(hp):
        for a, (ref, _) in enumerate(arrays[:2]):
            for nb in (1, 2):
                forwards[h, a, 0, nb] = send(
                    ref.at[:, :, head_cols(slot * hp + h)], bufs[a].at[h, nb, slot], groups[2 - nb])
            fwd_base[h, a] = reserve(6)

    def order_at(t):
        return lax.rem(t + 1, 3) + 1

    def forward(h, a, t):
        s = lax.rem(slot + 4 - order_at(t), 4)
        remote(bufs[a].at[h, 0, s], bufs[a].at[h, 0, s], far(1), in_base[h, a] + t).wait_recv()
        for nb in (1, 2):
            remote(bufs[a].at[h, 0, s], bufs[a].at[h, nb, s], groups[2 - nb], fwd_base[h, a] + t * 2 + nb - 1).start()

    def forwards_done(h, a, recv):
        for nb in (1, 2):
            if recv:
                forwards[h, a, 0, nb].wait_recv()
            for t in range(3):
                copy = remote(bufs[a].at[h, 0, 0], bufs[a].at[h, nb, 0], groups[2 - nb], fwd_base[h, a] + t * 2 + nb - 1)
                if recv:
                    copy.wait_recv()
                else:
                    copy.wait_send()

    def make_bias():
        bias_g[...] = jnp.full(bias_g.shape, NEG, F32)

        @pl.loop(0, 4)
        def _(i):
            tile = i * quarter + rank
            query_of = pairs_sc[i, 0:1, :]
            key_of = pairs_sc[i, 1:2, :]
            near = [rank + quarter * s for s in range(4)] + [lax.rem(tile + 1, n), lax.rem(tile + n - 1, n)]
            for j, key_tile in enumerate(near):
                for c in range(blocks):
                    key_id = key_tile * blocks + c
                    for b in range(blocks):
                        hit = jnp.where((query_of == b) & (key_of == key_id), 1.0, 0.0)
                        hit = jnp.max(hit, axis=1, keepdims=True)
                        hit = jnp.maximum(hit, (tile * blocks + b == key_id).astype(F32))
                        value = jnp.where(hit > 0.5, 0.0, NEG)
                        at = j * tokens + c * BLOCK
                        bias_g[i, b:b + 1, at:at + BLOCK] = jnp.broadcast_to(value, (1, BLOCK))

    w_copy.wait()

    ahead = (rank == quarter - 1).astype(jnp.int32)
    behind = 3 * (rank == 0).astype(jnp.int32)
    halo = {0: {}, 1: {}}
    edges = {}

    def halo_main(a, h):
        buf = vv.at[h, 0] if a == 0 else gg.at[h]
        halo[a][h] = [
            send(buf.at[:, :, pl.ds(first, 16)], slab.at[a, h, side, :, pl.ds(1, tx)], cols_of[side])
            for side, first in ((0, ty - 16), (1, 0))
        ]

    def halo_edges(a, h):
        for e, x in ((1, tx + 1), (2, 0)):
            if a == 0:
                row = vv.at[h, e, :, 0 if e == 1 else tx - 1]
            else:
                row = gedge.at[h, e - 1]
            for side, first in ((0, ty - 16), (1, 0)):
                halo[a][h].append(send(row.at[:, pl.ds(first, 16)], slab.at[a, h, side, :, x], cols_of[side]))

    def arrive_v(h):
        mine[h, V].wait()
        halo_main(0, h)

    def arrive_g(h):
        for d in ORDER:
            incoming[h, G, d].wait_recv()
        mine[h, G].wait()
        edges[h] = [send(gg.at[h, :, tx - 1], gedge.at[h, 1], next_group),
                    send(gg.at[h, :, 0], gedge.at[h, 0], prev_group)]
        halo_main(1, h)

    def arrive_rest(h):
        forwards_done(h, V, True)
        halo_edges(0, h)
        for d in ORDER:
            incoming[h, Q, d].wait_recv()
        for copy in edges[h]:
            copy.wait_recv()
        halo_edges(1, h)
        forwards_done(h, K, True)
        mine[h, K].wait()
        mine[h, Q].wait()

    has_left = (col > 0).astype(F32)
    has_right = (col < m - 1).astype(F32)

    def conv_tile(a, h, i):
        tile = i * quarter + rank
        has_up = (tile > 0).astype(F32)
        has_down = (tile < n - 1).astype(F32)
        above = lax.rem(i + behind, 4)
        below = lax.rem(i + ahead, 4)
        cols = head_cols(slot * hp + h)
        row_id = lax.broadcasted_iota(jnp.int32, (ty, HD), 0)
        sums = [None] * tx
        for x in range(tx + 2):
            if x == 0:
                row = (vv[h, 2, above, tx - 1] if a == 0 else gedge[h, 1, above]).astype(F32) * has_up
                at = above
            elif x == tx + 1:
                row = (vv[h, 1, below, 0] if a == 0 else gedge[h, 0, below]).astype(F32) * has_down
                at = below
            else:
                row = (vv[h, 0, i, x - 1] if a == 0 else gg[h, i, x - 1]).astype(F32)
                at = i
            left = slab[a, h, 0, at, x].astype(F32)[15:16] * has_left
            right = slab[a, h, 1, at, x].astype(F32)[0:1] * has_right
            if x == 0:
                left, right = left * has_up, right * has_up
            if x == tx + 1:
                left, right = left * has_down, right * has_down
            shifted = (
                jnp.where(row_id == 0, left, pltpu.roll(row, 1, 0)),
                row,
                jnp.where(row_id == ty - 1, right, pltpu.roll(row, ty - 1, 0)),
            )
            for step in (-1, 0, 1):
                target = x - 1 - step
                if 0 <= target < tx:
                    for b in range(3):
                        tap = 3 * (step + 1) + b
                        tap = tap if a == 0 else 8 - tap
                        term = w_sc[pl.ds(tap, 1), cols] * shifted[b]
                        sums[target] = term if sums[target] is None else sums[target] + term
        return jnp.concatenate(sums, axis=0)

    nt = (((1,), (1,)), ((), ()))
    nn = (((1,), (0,)), ((), ()))
    tn = (((0,), (0,)), ((), ()))

    def dot(x, y, dims):
        return lax.dot_general(x, y, dims, preferred_element_type=F32)

    def flat(x):
        return x.reshape(tokens, HD)

    back_base = {}

    def give_back(a, h, t, i):
        cols = head_cols(slot * hp + h)

        @pl.when(t < 3)
        def _():
            remote(res.at[a, h, i], outputs[a].at[:, :, cols], {"gx": i * quarter + rank}, back_base[a, h] + t).start()

    def keep(a, h):
        return local(res.at[a, h, slot], outputs[a].at[:, :, head_cols(slot * hp + h)])

    part_base = {}

    def attend(h):
        back_base[1, h] = reserve(3)
        part_base[h] = reserve(16)
        dk_acc[...] = jnp.zeros(dk_acc.shape, F32)
        dv_acc[...] = jnp.zeros(dv_acc.shape, F32)

        @pl.loop(0, 4)
        def _(t):
            i = lax.rem(slot + lax.rem(t + 1, 3) + 1, 4)
            i = lax.select(t == 3, slot, i)
            q = flat(qg[h, i])
            g = flat(gg[h, i])
            keys = [(0, 0), (0, 1), (0, 2), (0, 3), (1, lax.rem(i + ahead, 4)), (2, lax.rem(i + behind, 4))]
            top = None
            for j, (nb, s) in enumerate(keys):
                js = pl.ds(j * tokens, tokens)
                score = dot(q, flat(kk[h, nb, s]), nt)
                bias = bias_g[i, :, js]
                parts = [score[b * BLOCK:(b + 1) * BLOCK] + bias[b:b + 1] for b in range(blocks)]
                score = jnp.concatenate(parts, axis=0)
                s_sc[:, js] = score
                peak = jnp.max(score, axis=1, keepdims=True)
                top = peak if top is None else jnp.maximum(top, peak)
            total = jnp.zeros((tokens, 1), F32)
            out = jnp.zeros((tokens, HD), F32)
            for j, (nb, s) in enumerate(keys):
                js = pl.ds(j * tokens, tokens)
                prob = jnp.exp2((s_sc[:, js] - top) * (SCALE * LOG2E))
                s_sc[:, js] = prob
                total = total + jnp.sum(prob, axis=1, keepdims=True)
                out = out + dot(prob.astype(BF16), flat(vv[h, nb, s]), nn)
            inv = 1.0 / total
            out = out * inv
            o_acc[i] = out
            grad_dot = jnp.sum(g.astype(F32) * out, axis=1, keepdims=True)
            dq = jnp.zeros((tokens, HD), F32)
            for j, (nb, s) in enumerate(keys):
                js = pl.ds(j * tokens, tokens)
                prob_grad = dot(g, flat(vv[h, nb, s]), nt)
                prob = s_sc[:, js] * inv
                score_grad = (prob * (prob_grad - grad_dot)).astype(BF16)
                dq = dq + dot(score_grad, flat(kk[h, nb, s]), nn)
                dk = dot(score_grad, q, tn)
                dv = dot(prob.astype(BF16), g, tn)
                if nb == 0:
                    dk_acc[s] += dk
                    dv_acc[s] += dv
                else:
                    for a, value in enumerate((dk, dv)):
                        part_send[a, h, nb - 1, s] = value.astype(BF16).reshape(tx, ty, HD)
                        remote(part_send.at[a, h, nb - 1, s], part_recv.at[a, h, nb - 1, s], groups[nb - 1],
                               part_base[h] + t * 4 + a * 2 + nb - 1).start()
            res[1, h, i] = (dq * SCALE).astype(BF16).reshape(tx, ty, HD)
            give_back(1, h, t, i)
            if h + 1 < hp:

                @pl.when(t < 3)
                def _():
                    forward(h + 1, K, t)
                    forward(h + 1, V, t)

        kept.append(keep(1, h))

    def tile_at(t):
        return lax.select(t == 3, slot, lax.rem(slot + lax.rem(t + 1, 3) + 1, 4))

    def finish_out(h):
        for copy in halo[0][h]:
            copy.wait_recv()
        back_base[0, h] = reserve(3)

        @pl.loop(0, 4)
        def _(t):
            i = tile_at(t)
            res[0, h, i] = (o_acc[i] + conv_tile(0, h, i)).astype(BF16).reshape(tx, ty, HD)
            give_back(0, h, t, i)

        kept.append(keep(0, h))

    def part_copy(h, t, a, nb):
        return remote(part_send.at[a, h, nb, 0], part_recv.at[a, h, nb, 0], groups[nb], part_base[h] + t * 4 + a * 2 + nb)

    def finish_grads(h):
        for t in range(4):
            for a in range(2):
                for nb in range(2):
                    part_copy(h, t, a, nb).wait_recv()
        for copy in halo[1][h]:
            copy.wait_recv()
        back_base[2, h] = reserve(3)
        back_base[3, h] = reserve(3)

        @pl.loop(0, 4)
        def _(t):
            s = tile_at(t)
            for a, acc in enumerate((dk_acc, dv_acc)):
                value = acc[s] + flat(part_recv[a, h, 0, s]).astype(F32) + flat(part_recv[a, h, 1, s]).astype(F32)
                value = value * SCALE if a == 0 else value + conv_tile(1, h, s)
                res[2 + a, h, s] = value.astype(BF16).reshape(tx, ty, HD)
                give_back(2 + a, h, t, s)

        kept.append(keep(2, h))
        kept.append(keep(3, h))

    kept = []
    pairs_copy.wait()
    for copy in pairs_copies:
        copy.wait_recv()
    make_bias()
    for t in range(3):
        forward(0, K, t)
    for t in range(3):
        forward(0, V, t)
    for h in range(hp):
        arrive_v(h)
        arrive_g(h)
        arrive_rest(h)
        attend(h)
        finish_out(h)
        finish_grads(h)

    for copy in kept:
        copy.wait()
    for a in range(4):
        for h in range(hp):
            for t in range(3):
                copy = remote(res.at[a, h, 0], outputs[a].at[:, :, head_cols(slot * hp + h)], far(1), back_base[a, h] + t)
                copy.wait_recv()
                copy.wait_send()
    for h in range(hp):
        for a in range(2):
            forwards_done(h, a, False)
            for t in range(4):
                for nb in range(2):
                    part_copy(h, t, a, nb).wait_send()
    for copy in sent:
        copy.wait_send()


def hand_over(*refs):
    count = (len(refs) - 2) // 2
    sources, targets = refs[:count], refs[count:2 * count]
    stage, sems = refs[2 * count:]
    first = [pltpu.make_async_copy(sources[a], stage.at[a], sems.at[0, a]) for a in range(count)]
    second = [pltpu.make_async_copy(stage.at[a], targets[a], sems.at[1, a]) for a in range(count)]
    for copy in first:
        copy.start()
    for a in range(count):
        first[a].wait()
        second[a].start()
    for copy in second:
        copy.wait()


def per_device(n, m, queries, key_tokens, value_tokens, out_grad, conv_weight, block_pairs):
    tx, ty, width = queries.shape
    heads = width // HD
    hp = heads // 4
    tokens = tx * ty
    pairs = block_pairs.shape[2]
    vmem = pl.BlockSpec(memory_space=pltpu.VMEM)
    anywhere = pl.BlockSpec(memory_space=pl.ANY)
    shape = jax.ShapeDtypeStruct(queries.shape, BF16)
    outs = pl.pallas_call(
        functools.partial(kernel, n, m, tx, ty),
        out_shape=(shape,) * 4,
        in_specs=[anywhere] * 6,
        out_specs=(anywhere,) * 4,
        scratch_shapes=[
            pltpu.VMEM((hp, 4, tx, ty, HD), BF16),
            pltpu.VMEM((hp, 4, tx, ty, HD), BF16),
            pltpu.VMEM((hp, 3, 4, tx, ty, HD), BF16),
            pltpu.VMEM((hp, 3, 4, tx, ty, HD), BF16),
            pltpu.VMEM((4, 8, 6 * tokens), F32),
            pltpu.VMEM((tokens, 6 * tokens), F32),
            pltpu.VMEM((4, tokens, HD), F32),
            pltpu.VMEM((4, tokens, HD), F32),
            pltpu.VMEM((4, tokens, HD), F32),
            pltpu.VMEM((2, hp, 2, 4, tx, ty, HD), BF16),
            pltpu.VMEM((2, hp, 2, 4, tx, ty, HD), BF16),
            pltpu.VMEM((4, hp, 4, tx, ty, HD), BF16),
            pltpu.VMEM((hp, 2, 4, ty, HD), BF16),
            pltpu.VMEM((2, hp, 2, 4, tx + 2, 16, HD), BF16),
            pltpu.VMEM((9, width), F32),
            pltpu.VMEM((4, 2, pairs), jnp.int32),
            pltpu.SemaphoreType.DMA((160,)),
            pltpu.SemaphoreType.DMA((160,)),
            pltpu.SemaphoreType.DMA((8 * hp + 2,)),
        ],
        compiler_params=pltpu.CompilerParams(
            collective_id=0, has_side_effects=True, vmem_limit_bytes=60 * 1024 * 1024
        ),
    )(queries, key_tokens, value_tokens, out_grad, conv_weight, block_pairs[0, 0].T)
    return pl.pallas_call(
        hand_over,
        out_shape=(shape,) * 4,
        in_specs=[anywhere] * 4,
        out_specs=(anywhere,) * 4,
        scratch_shapes=[pltpu.VMEM((4, tx, ty, width), BF16), pltpu.SemaphoreType.DMA((2, 4))],
    )(*outs)


def solution(mesh):
    grid = P("gx", "gy", None)
    return jax.shard_map(
        functools.partial(per_device, mesh.shape["gx"], mesh.shape["gy"]),
        mesh=mesh,
        in_specs=(grid, grid, grid, grid, P(), P("gx", "gy", None, None)),
        out_specs=(grid, grid, grid, grid),
        check_vma=False,
    )
```

```python
import functools
import math

import jax
import jax.numpy as jnp
from jax import lax
from jax.experimental import pallas as pl
from jax.experimental.pallas import tpu as pltpu
from jax.sharding import PartitionSpec as P

HD = 128
BLOCK = 128
NEG = -1e30
MESH = pl.DeviceIdType.MESH
SCALE = 1.0 / math.sqrt(HD)
LOG2E = math.log2(math.e)
F32 = jnp.float32
BF16 = jnp.bfloat16
ORDER = (2, 3, 1)


def kernel(
    n, m, tx, ty,
    q_ref, k_ref, v_ref, g_ref, w_ref, pairs_ref,
    o_ref, dq_ref, dk_ref, dv_ref,
    qg, gg, kk, vv, bias_g, s_sc, o_acc, dk_acc, dv_acc,
    part_send, part_recv, res, gedge, slab, w_sc, pairs_sc,
    send_sem, recv_sem, local_sem,
):
    tokens = tx * ty
    blocks = tokens // BLOCK
    heads = q_ref.shape[2] // HD
    hp = heads // 4
    quarter = n // 4
    own = lax.axis_index("gx")
    col = lax.axis_index("gy")
    slot = own // quarter
    rank = lax.rem(own, quarter)
    outputs = (o_ref, dq_ref, dk_ref, dv_ref)

    def far(d):
        return {"gx": lax.rem(own + d * quarter, n)}

    next_group = {"gx": slot * quarter + lax.rem(rank + 1, quarter)}
    prev_group = {"gx": slot * quarter + lax.rem(rank + quarter - 1, quarter)}
    groups = (next_group, prev_group)
    next_col = {"gy": lax.rem(col + 1, m)}
    prev_col = {"gy": lax.rem(col + m - 1, m)}
    cols_of = (next_col, prev_col)

    barrier = pltpu.get_barrier_semaphore()
    partners = [far(1), far(2), far(3), next_group, prev_group, next_col, prev_col]
    for partner in partners:
        pl.semaphore_signal(barrier, inc=1, device_id=partner, device_id_type=MESH)

    count = [0]
    sent = []
    local_count = [0]

    def reserve(k):
        at = count[0]
        count[0] += k
        return at

    def remote(src, dst, device, at):
        return pltpu.make_async_remote_copy(
            src_ref=src, dst_ref=dst, send_sem=send_sem.at[at], recv_sem=recv_sem.at[at],
            device_id=device, device_id_type=MESH,
        )

    def send(src, dst, device):
        copy = remote(src, dst, device, reserve(1))
        copy.start()
        sent.append(copy)
        return copy

    def local(src, dst):
        copy = pltpu.make_async_copy(src, dst, local_sem.at[local_count[0]])
        local_count[0] += 1
        copy.start()
        return copy

    def head_cols(head):
        return pl.ds(pl.multiple_of(head * HD, HD), HD)

    pairs_copy = local(pairs_ref, pairs_sc.at[slot])
    w_copy = local(w_ref, w_sc)
    K, V, G, Q = 0, 1, 2, 3
    arrays = ((k_ref, lambda h, s: kk.at[h, 0, s]), (v_ref, lambda h, s: vv.at[h, 0, s]),
              (g_ref, lambda h, s: gg.at[h, s]), (q_ref, lambda h, s: qg.at[h, s]))
    mine = {}
    for h in range(hp):
        for a, (ref, place) in enumerate(arrays):
            mine[h, a] = local(ref.at[:, :, head_cols(slot * hp + h)], place(h, slot))

    pl.semaphore_wait(barrier, len(partners))

    pairs_copies = [send(pairs_ref, pairs_sc.at[slot], far(d)) for d in ORDER]
    incoming = {}
    in_base = {}
    for h in range(hp):
        for a, (ref, place) in enumerate(arrays):
            in_base[h, a] = count[0]
            for d in ORDER:
                target = lax.rem(slot + d, 4)
                incoming[h, a, d] = send(ref.at[:, :, head_cols(target * hp + h)], place(h, slot), far(d))

    forwards = {}
    fwd_base = {}
    bufs = (kk, vv)
    for h in range(hp):
        for a, (ref, _) in enumerate(arrays[:2]):
            for nb in (1, 2):
                forwards[h, a, 0, nb] = send(
                    ref.at[:, :, head_cols(slot * hp + h)], bufs[a].at[h, nb, slot], groups[2 - nb])
            fwd_base[h, a] = reserve(6)

    def order_at(t):
        return lax.rem(t + 1, 3) + 1

    def forward(h, a, t):
        s = lax.rem(slot + 4 - order_at(t), 4)
        remote(bufs[a].at[h, 0, s], bufs[a].at[h, 0, s], far(1), in_base[h, a] + t).wait_recv()
        for nb in (1, 2):
            remote(bufs[a].at[h, 0, s], bufs[a].at[h, nb, s], groups[2 - nb], fwd_base[h, a] + t * 2 + nb - 1).start()

    def forwards_done(h, a, recv):
        for nb in (1, 2):
            if recv:
                forwards[h, a, 0, nb].wait_recv()
            for t in range(3):
                copy = remote(bufs[a].at[h, 0, 0], bufs[a].at[h, nb, 0], groups[2 - nb], fwd_base[h, a] + t * 2 + nb - 1)
                if recv:
                    copy.wait_recv()
                else:
                    copy.wait_send()

    def make_bias():
        bias_g[...] = jnp.full(bias_g.shape, NEG, F32)

        @pl.loop(0, 4)
        def _(i):
            tile = i * quarter + rank
            query_of = pairs_sc[i, 0:1, :]
            key_of = pairs_sc[i, 1:2, :]
            near = [rank + quarter * s for s in range(4)] + [lax.rem(tile + 1, n), lax.rem(tile + n - 1, n)]
            for j, key_tile in enumerate(near):
                for c in range(blocks):
                    key_id = key_tile * blocks + c
                    for b in range(blocks):
                        hit = jnp.where((query_of == b) & (key_of == key_id), 1.0, 0.0)
                        hit = jnp.max(hit, axis=1, keepdims=True)
                        hit = jnp.maximum(hit, (tile * blocks + b == key_id).astype(F32))
                        value = jnp.where(hit > 0.5, 0.0, NEG)
                        at = j * tokens + c * BLOCK
                        bias_g[i, b:b + 1, at:at + BLOCK] = jnp.broadcast_to(value, (1, BLOCK))

    w_copy.wait()

    ahead = (rank == quarter - 1).astype(jnp.int32)
    behind = 3 * (rank == 0).astype(jnp.int32)
    halo = {0: {}, 1: {}}
    edges = {}

    def halo_main(a, h):
        buf = vv.at[h, 0] if a == 0 else gg.at[h]
        halo[a][h] = [
            send(buf.at[:, :, pl.ds(first, 16)], slab.at[a, h, side, :, pl.ds(1, tx)], cols_of[side])
            for side, first in ((0, ty - 16), (1, 0))
        ]

    def halo_edges(a, h):
        for e, x in ((1, tx + 1), (2, 0)):
            if a == 0:
                row = vv.at[h, e, :, 0 if e == 1 else tx - 1]
            else:
                row = gedge.at[h, e - 1]
            for side, first in ((0, ty - 16), (1, 0)):
                halo[a][h].append(send(row.at[:, pl.ds(first, 16)], slab.at[a, h, side, :, x], cols_of[side]))

    def arrive_v(h):
        mine[h, V].wait()
        halo_main(0, h)

    def arrive_g(h):
        for d in ORDER:
            incoming[h, G, d].wait_recv()
        mine[h, G].wait()
        edges[h] = [send(gg.at[h, :, tx - 1], gedge.at[h, 1], next_group),
                    send(gg.at[h, :, 0], gedge.at[h, 0], prev_group)]
        halo_main(1, h)

    def arrive_rest(h):
        forwards_done(h, V, True)
        halo_edges(0, h)
        for d in ORDER:
            incoming[h, Q, d].wait_recv()
        for copy in edges[h]:
            copy.wait_recv()
        halo_edges(1, h)
        forwards_done(h, K, True)
        mine[h, K].wait()
        mine[h, Q].wait()

    has_left = (col > 0).astype(F32)
    has_right = (col < m - 1).astype(F32)

    def conv_tile(a, h, i):
        tile = i * quarter + rank
        has_up = (tile > 0).astype(F32)
        has_down = (tile < n - 1).astype(F32)
        above = lax.rem(i + behind, 4)
        below = lax.rem(i + ahead, 4)
        cols = head_cols(slot * hp + h)
        row_id = lax.broadcasted_iota(jnp.int32, (ty, HD), 0)
        sums = [None] * tx
        for x in range(tx + 2):
            if x == 0:
                row = (vv[h, 2, above, tx - 1] if a == 0 else gedge[h, 1, above]).astype(F32) * has_up
                at = above
            elif x == tx + 1:
                row = (vv[h, 1, below, 0] if a == 0 else gedge[h, 0, below]).astype(F32) * has_down
                at = below
            else:
                row = (vv[h, 0, i, x - 1] if a == 0 else gg[h, i, x - 1]).astype(F32)
                at = i
            left = slab[a, h, 0, at, x].astype(F32)[15:16] * has_left
            right = slab[a, h, 1, at, x].astype(F32)[0:1] * has_right
            if x == 0:
                left, right = left * has_up, right * has_up
            if x == tx + 1:
                left, right = left * has_down, right * has_down
            shifted = (
                jnp.where(row_id == 0, left, pltpu.roll(row, 1, 0)),
                row,
                jnp.where(row_id == ty - 1, right, pltpu.roll(row, ty - 1, 0)),
            )
            for step in (-1, 0, 1):
                target = x - 1 - step
                if 0 <= target < tx:
                    for b in range(3):
                        tap = 3 * (step + 1) + b
                        tap = tap if a == 0 else 8 - tap
                        term = w_sc[pl.ds(tap, 1), cols] * shifted[b]
                        sums[target] = term if sums[target] is None else sums[target] + term
        return jnp.concatenate(sums, axis=0)

    nt = (((1,), (1,)), ((), ()))
    nn = (((1,), (0,)), ((), ()))
    tn = (((0,), (0,)), ((), ()))

    def dot(x, y, dims):
        return lax.dot_general(x, y, dims, preferred_element_type=F32)

    def flat(x):
        return x.reshape(tokens, HD)

    back_base = {}

    def give_back(a, h, t, i):
        cols = head_cols(slot * hp + h)

        @pl.when(t < 3)
        def _():
            remote(res.at[a, h, i], outputs[a].at[:, :, cols], {"gx": i * quarter + rank}, back_base[a, h] + t).start()

    def keep(a, h):
        return local(res.at[a, h, slot], outputs[a].at[:, :, head_cols(slot * hp + h)])

    part_base = {}

    def attend(h):
        back_base[1, h] = reserve(3)
        part_base[h] = reserve(16)
        dk_acc[...] = jnp.zeros(dk_acc.shape, F32)
        dv_acc[...] = jnp.zeros(dv_acc.shape, F32)

        @pl.loop(0, 4)
        def _(t):
            i = lax.rem(slot + lax.rem(t + 1, 3) + 1, 4)
            i = lax.select(t == 3, slot, i)
            q = flat(qg[h, i])
            g = flat(gg[h, i])
            keys = [(0, 0), (0, 1), (0, 2), (0, 3), (1, lax.rem(i + ahead, 4)), (2, lax.rem(i + behind, 4))]
            top = None
            for j, (nb, s) in enumerate(keys):
                js = pl.ds(j * tokens, tokens)
                score = dot(q, flat(kk[h, nb, s]), nt)
                bias = bias_g[i, :, js]
                parts = [score[b * BLOCK:(b + 1) * BLOCK] + bias[b:b + 1] for b in range(blocks)]
                score = jnp.concatenate(parts, axis=0)
                s_sc[:, js] = score
                peak = jnp.max(score, axis=1, keepdims=True)
                top = peak if top is None else jnp.maximum(top, peak)
            total = jnp.zeros((tokens, 1), F32)
            out = jnp.zeros((tokens, HD), F32)
            for j, (nb, s) in enumerate(keys):
                js = pl.ds(j * tokens, tokens)
                prob = jnp.exp2((s_sc[:, js] - top) * (SCALE * LOG2E))
                s_sc[:, js] = prob
                total = total + jnp.sum(prob, axis=1, keepdims=True)
                out = out + dot(prob.astype(BF16), flat(vv[h, nb, s]), nn)
            inv = 1.0 / total
            out = out * inv
            o_acc[i] = out
            grad_dot = jnp.sum(g.astype(F32) * out, axis=1, keepdims=True)
            dq = jnp.zeros((tokens, HD), F32)
            for j, (nb, s) in enumerate(keys):
                js = pl.ds(j * tokens, tokens)
                prob_grad = dot(g, flat(vv[h, nb, s]), nt)
                prob = s_sc[:, js] * inv
                score_grad = (prob * (prob_grad - grad_dot)).astype(BF16)
                dq = dq + dot(score_grad, flat(kk[h, nb, s]), nn)
                dk = dot(score_grad, q, tn)
                dv = dot(prob.astype(BF16), g, tn)
                if nb == 0:
                    dk_acc[s] += dk
                    dv_acc[s] += dv
                else:
                    for a, value in enumerate((dk, dv)):
                        part_send[a, h, nb - 1, s] = value.astype(BF16).reshape(tx, ty, HD)
                        remote(part_send.at[a, h, nb - 1, s], part_recv.at[a, h, nb - 1, s], groups[nb - 1],
                               part_base[h] + t * 4 + a * 2 + nb - 1).start()
            res[1, h, i] = (dq * SCALE).astype(BF16).reshape(tx, ty, HD)
            give_back(1, h, t, i)
            if h + 1 < hp:

                @pl.when(t < 3)
                def _():
                    forward(h + 1, K, t)
                    forward(h + 1, V, t)

        kept.append(keep(1, h))

    def tile_at(t):
        return lax.select(t == 3, slot, lax.rem(slot + lax.rem(t + 1, 3) + 1, 4))

    def finish_out(h):
        for copy in halo[0][h]:
            copy.wait_recv()
        back_base[0, h] = reserve(3)

        @pl.loop(0, 4)
        def _(t):
            i = tile_at(t)
            res[0, h, i] = (o_acc[i] + conv_tile(0, h, i)).astype(BF16).reshape(tx, ty, HD)
            give_back(0, h, t, i)

        kept.append(keep(0, h))

    def part_copy(h, t, a, nb):
        return remote(part_send.at[a, h, nb, 0], part_recv.at[a, h, nb, 0], groups[nb], part_base[h] + t * 4 + a * 2 + nb)

    def finish_grads(h):
        for t in range(4):
            for a in range(2):
                for nb in range(2):
                    part_copy(h, t, a, nb).wait_recv()
        for copy in halo[1][h]:
            copy.wait_recv()
        back_base[2, h] = reserve(3)
        back_base[3, h] = reserve(3)

        @pl.loop(0, 4)
        def _(t):
            s = tile_at(t)
            for a, acc in enumerate((dk_acc, dv_acc)):
                value = acc[s] + flat(part_recv[a, h, 0, s]).astype(F32) + flat(part_recv[a, h, 1, s]).astype(F32)
                value = value * SCALE if a == 0 else value + conv_tile(1, h, s)
                res[2 + a, h, s] = value.astype(BF16).reshape(tx, ty, HD)
                give_back(2 + a, h, t, s)

        kept.append(keep(2, h))
        kept.append(keep(3, h))

    kept = []
    pairs_copy.wait()
    for copy in pairs_copies:
        copy.wait_recv()
    make_bias()
    for t in range(3):
        forward(0, K, t)
    for t in range(3):
        forward(0, V, t)
    for h in range(hp):
        arrive_v(h)
        arrive_g(h)
        arrive_rest(h)
        attend(h)
        finish_out(h)
        finish_grads(h)

    for copy in kept:
        copy.wait()
    for a in range(4):
        for h in range(hp):
            for t in range(3):
                copy = remote(res.at[a, h, 0], outputs[a].at[:, :, head_cols(slot * hp + h)], far(1), back_base[a, h] + t)
                copy.wait_recv()
                copy.wait_send()
    for h in range(hp):
        for a in range(2):
            forwards_done(h, a, False)
            for t in range(4):
                for nb in range(2):
                    part_copy(h, t, a, nb).wait_send()
    for copy in sent:
        copy.wait_send()


def hand_over(*refs):
    count = (len(refs) - 1) // 2
    sources, targets, sems = refs[:count], refs[count:2 * count], refs[-1]
    copies = [pltpu.make_async_copy(sources[a], targets[a], sems.at[a]) for a in range(count)]
    for copy in copies:
        copy.start()
    for copy in copies:
        copy.wait()


def per_device(n, m, queries, key_tokens, value_tokens, out_grad, conv_weight, block_pairs):
    tx, ty, width = queries.shape
    heads = width // HD
    hp = heads // 4
    tokens = tx * ty
    pairs = block_pairs.shape[2]
    vmem = pl.BlockSpec(memory_space=pltpu.VMEM)
    anywhere = pl.BlockSpec(memory_space=pl.ANY)
    shape = jax.ShapeDtypeStruct(queries.shape, BF16)
    outs = pl.pallas_call(
        functools.partial(kernel, n, m, tx, ty),
        out_shape=(pltpu.VMEM(queries.shape, BF16),) * 4,
        in_specs=[anywhere] * 6,
        out_specs=(vmem,) * 4,
        scratch_shapes=[
            pltpu.VMEM((hp, 4, tx, ty, HD), BF16),
            pltpu.VMEM((hp, 4, tx, ty, HD), BF16),
            pltpu.VMEM((hp, 3, 4, tx, ty, HD), BF16),
            pltpu.VMEM((hp, 3, 4, tx, ty, HD), BF16),
            pltpu.VMEM((4, 8, 6 * tokens), F32),
            pltpu.VMEM((tokens, 6 * tokens), F32),
            pltpu.VMEM((4, tokens, HD), F32),
            pltpu.VMEM((4, tokens, HD), F32),
            pltpu.VMEM((4, tokens, HD), F32),
            pltpu.VMEM((2, hp, 2, 4, tx, ty, HD), BF16),
            pltpu.VMEM((2, hp, 2, 4, tx, ty, HD), BF16),
            pltpu.VMEM((4, hp, 4, tx, ty, HD), BF16),
            pltpu.VMEM((hp, 2, 4, ty, HD), BF16),
            pltpu.VMEM((2, hp, 2, 4, tx + 2, 16, HD), BF16),
            pltpu.VMEM((9, width), F32),
            pltpu.VMEM((4, 2, pairs), jnp.int32),
            pltpu.SemaphoreType.DMA((160,)),
            pltpu.SemaphoreType.DMA((160,)),
            pltpu.SemaphoreType.DMA((8 * hp + 2,)),
        ],
        compiler_params=pltpu.CompilerParams(
            collective_id=0, has_side_effects=True, vmem_limit_bytes=64500000
        ),
    )(queries, key_tokens, value_tokens, out_grad, conv_weight, block_pairs[0, 0].T)
    return pl.pallas_call(
        hand_over,
        out_shape=(shape,) * 4,
        in_specs=[vmem] * 4,
        out_specs=(anywhere,) * 4,
        scratch_shapes=[pltpu.SemaphoreType.DMA((4,))],
        compiler_params=pltpu.CompilerParams(vmem_limit_bytes=4 * 1024 * 1024),
    )(*outs)


def solution(mesh):
    grid = P("gx", "gy", None)
    return jax.shard_map(
        functools.partial(per_device, mesh.shape["gx"], mesh.shape["gy"]),
        mesh=mesh,
        in_specs=(grid, grid, grid, grid, P(), P("gx", "gy", None, None)),
        out_specs=(grid, grid, grid, grid),
        check_vma=False,
    )
```
